32 devices in a mesh: dp: 2 (over x), row: 4 (over z), col: 4 (over y, core).
Axes of the slice: x: 2, y: 2, z: 4, core: 2. Of those that a mesh axis runs over, the one named last changes fastest.
Arguments:
- layer_input: bfloat16 [4096, 1152], P(('dp', 'col'), 'row'), may hold values from -6 to 6
- block_ids: int32 [2, 2048], P('dp', ('row', 'col')), may hold values from 0 to 31, never falling along the last dimension, each value on 1 to 512 neighbouring positions
- positions: int32 [2, 2048], P('dp', ('row', 'col')), may hold values from 0 to 2047
- norm_attn: float32 [2, 1152], P(None, 'row'), may hold values from 0.5 to 1.5
- w_qkv: bfloat16 [2, 1152, 1920], P(None, 'row', 'col'), may hold values from -0.1875 to 0.1875
- w_out: bfloat16 [2, 1152, 1152], P(None, 'col', 'row'), may hold values from -0.75 to 0.75
- norm_ffn: float32 [2, 1152], P(None, 'row'), may hold values from 0.5 to 1.5
- w_gate_up: bfloat16 [2, 1152, 2, 3072], P(None, 'row', None, 'col'), may hold values from -0.1875 to 0.1875
- w_down: bfloat16 [2, 3072, 1152], P(None, 'col', 'row'), may hold values from -0.109375 to 0.109375
- cotangent: bfloat16 [4096, 1152], P(('dp', 'col'), 'row'), may hold values from -6 to 6
Outputs:
- activations: bfloat16 [4096, 1152], P(('dp', 'col'), 'row')
- input_grad: float32 [4096, 1152], P(('dp', 'col'), 'row')
- grad_norm_attn: float32 [2, 1152], P(None, 'row')
- grad_qkv: float32 [2, 1152, 1920], P(None, 'row', 'col')
- grad_out: float32 [2, 1152, 1152], P(None, 'col', 'row')
- grad_norm_ffn: float32 [2, 1152], P(None, 'row')
- grad_gate_up: float32 [2, 1152, 2, 3072], P(None, 'row', None, 'col')
- grad_down: float32 [2, 3072, 1152], P(None, 'col', 'row')
The draws below stay inside these ranges and needn't reach their ends.
Inputs may be any that keep to these rules, and one draw needn't show every extreme that they name: `block_ids`: in each sequence the ids never fall, and each id covers 1 to 512 consecutive tokens.
All inputs are finite; a program needn't handle non-finite values.
Results may differ from the reference program's by a relative error of at most 0.035.
Values may be sent and summed in bfloat16 or wider, within the bound.
No kernel may reach another device: no remote copies, remote signals or barrier semaphores. Data moves between devices by JAX's collectives and lax.ppermute only.
A program may use at most 192 MiB of HBM per device.

```python
import math
import jax
import jax.numpy as jnp
import numpy as np
from jax import lax

D = 1152
FF = 3072
HEADS = 18
KV_HEADS = 6
HEAD_DIM = 64
LAYERS = 2
SEQ = 2048
TOKENS = 4096
QKV = 1920
HD_ALL = 1152
N_DP = 2
N_ROW = 4
N_COL = 4


def set_ends(values, stream_key, least, high):
    shape = values.shape
    spot = [jax.random.randint(jax.random.fold_in(stream_key, axis), (), 0, shape[axis]) for axis in range(len(shape))]
    values = values.at[tuple(spot)].set(least)
    longest = shape.index(max(shape))
    spot[longest] = (spot[longest] + 1) % shape[longest]
    return values.at[tuple(spot)].set(high)


def level_of(stream_key, extent, split, least, high):
    level, own = 1.0, jax.random.fold_in(stream_key, 6)
    for dim, shards_of in split:
        heights = jnp.exp(jax.random.uniform(jax.random.fold_in(own, dim), (shards_of,), jnp.float32, least / len(split), high / len(split)))
        level = level * jnp.repeat(heights, extent[dim] // shards_of).reshape([-1 if axis == dim else 1 for axis in range(len(extent))])
    return level


def split_up(amount, total, limit, skew):
    portions = [(1 << 20) // math.isqrt(standing ** skew) + 1 for standing in range(2, amount + 1)]
    spare, holding = total - limit - (amount - 1), [1] * (amount - 1)
    while spare > 0:
        free = [i for i in range(amount - 1) if holding[i] < limit]
        pool, remaining = sum([portions[i] for i in free]), spare
        for i in free:
            extra = min(limit - holding[i], max(1, remaining * portions[i] // pool), spare)
            holding[i] = holding[i] + extra
            spare = spare - extra
    return np.array([limit] + holding)


def uneven(stream_key, count, total, limit, skew):
    if count == 2:
        one = jax.random.randint(stream_key, (), max(1, total - limit), min(limit, total - 1) + 1)
        return jnp.stack([one, total - one])
    tallies = jnp.asarray(split_up(count, total, limit, skew), jnp.int32)
    twos = (count - 1) // 2
    source_of, sink = tallies[1:1 + 2 * twos:2], tallies[2:2 + 2 * twos:2]
    margin = jnp.minimum(source_of - 1, limit - sink)
    shifted = jax.random.randint(jax.random.fold_in(stream_key, 1), (twos,), 0, 1 << 20) % (margin + 1)
    tallies = tallies.at[1:1 + 2 * twos:2].set(source_of - shifted).at[2:2 + 2 * twos:2].set(sink + shifted)
    return tallies[jax.random.permutation(jax.random.fold_in(stream_key, 2), count)]


def centred(stream_key, shape, scale, most, split=(), kind=jnp.bfloat16):
    entries = jax.random.normal(stream_key, shape, jnp.float32) * scale
    if len(split) > 0:
        entries = level_of(stream_key, shape, split, -0.22, 0.18) * entries
    return jnp.clip(entries, min=-most, max=most).astype(kind)


def setup_inputs(seed: int = 0) -> dict:
    key_list = jax.random.split(jax.random.key(seed), 11)
    layer_input = centred(key_list[0], (TOKENS, D), 1.0, 6.0, ((0, 8), (1, 4)))
    block_ids = jax.vmap(lambda own: jnp.searchsorted(jnp.cumsum(uneven(own, 2 * N_ROW * N_COL, SEQ, SEQ // 4, 2)), jnp.arange(SEQ), side="right"))(jax.random.split(key_list[1], N_DP)).reshape((N_DP, SEQ)).astype(jnp.int32)
    positions = set_ends(jax.random.randint(key_list[2], (N_DP, SEQ), 0, SEQ), jax.random.fold_in(key_list[2], 1), 0, SEQ - 1).astype(jnp.int32)
    norm_attn = jnp.clip(1.0 + 0.1 * jax.random.normal(key_list[3], (LAYERS, D), jnp.float32), 0.5, 1.5)
    w_qkv = centred(key_list[4], (LAYERS, D, QKV), D ** -0.5, 0.1875, ((1, 4), (2, 4)))
    w_out = centred(key_list[5], (LAYERS, HD_ALL, D), (HD_ALL // 16) ** -0.5, 0.75, ((1, 4), (2, 4)))
    norm_ffn = jnp.clip(1.0 + 0.1 * jax.random.normal(key_list[6], (LAYERS, D), jnp.float32), 0.5, 1.5)
    w_gate_up = centred(key_list[7], (LAYERS, D, 2, FF), D ** -0.5, 0.1875, ((1, 4), (3, 4)))
    w_down = centred(key_list[8], (LAYERS, FF, D), FF ** -0.5, 0.109375, ((1, 4), (2, 4)))
    cotangent = centred(key_list[9], (TOKENS, D), 1.0, 6.0, ((0, 8), (1, 4)))
    return dict(layer_input=layer_input, block_ids=block_ids, positions=positions, norm_attn=norm_attn, w_qkv=w_qkv, w_out=w_out, norm_ffn=norm_ffn, w_gate_up=w_gate_up, w_down=w_down, cotangent=cotangent)


epsilon = 1e-05
rope_base = 10000.0
highest = lax.Precision.HIGHEST

@jax.custom_vjp
def low(v):
    return lax.optimization_barrier(v.astype(jnp.bfloat16)).astype(jnp.float32)

@jax.custom_vjp
def low_back(v):
    return v

def low_keep(v):
    return (low(v), None)

def low_pass(kept, grad):
    return (grad,)

def back_keep(v):
    return (v, None)

def back_low(kept, grad):
    return (low(grad),)
low.defvjp(low_keep, low_pass)
low_back.defvjp(back_keep, back_low)

def product(left, right):
    return jnp.dot(left, right, precision=highest)

def norm_rows(values, gain):
    factor = lax.rsqrt(lax.optimization_barrier(jnp.mean(values * values, axis=-1, keepdims=True)) + epsilon)
    return values * factor * gain

def angles(positions):
    freq_index = jnp.arange(HEAD_DIM // 2).astype(jnp.float32)
    freqs = rope_base ** (-2.0 * freq_index / HEAD_DIM)
    phase = positions.astype(jnp.float32)[:, None] * freqs[None, :]
    phase = jnp.concatenate([phase, phase], axis=-1)
    return (jnp.cos(phase)[:, None, :], jnp.sin(phase)[:, None, :])

def rotate(values, cosine, sine):
    half_dim = values.shape[-1] // 2
    turned = jnp.concatenate([-values[..., half_dim:], values[..., :half_dim]], axis=-1)
    return values * cosine + turned * sine

def attend(queries, keys, values, block_ids):
    group = HEADS // KV_HEADS
    length = queries.shape[0]
    block_len = min(512, length)
    query_blocks = queries.reshape(length // block_len, block_len, KV_HEADS, group, HEAD_DIM)
    id_blocks = block_ids.reshape(length // block_len, block_len)
    factor = HEAD_DIM ** (-0.5)

    @jax.checkpoint
    def one_block(block_item):
        query_block, query_ids = block_item
        scores = jnp.einsum('qhgd,khd->hgqk', query_block, keys, precision=highest) * factor
        allowed = block_ids[None, :] <= query_ids[:, None]
        scores = jnp.where(allowed, scores, -1e+30)
        row_max = lax.optimization_barrier(jnp.max(scores, axis=-1, keepdims=True))
        weights = jnp.where(allowed, jnp.exp(scores - row_max), 0.0)
        weights = weights / lax.optimization_barrier(jnp.sum(weights, axis=-1, keepdims=True))
        return jnp.einsum('hgqk,khd->qhgd', weights, values, precision=highest)
    result = lax.map(one_block, (query_blocks, id_blocks))
    return result.reshape(length, HEADS * HEAD_DIM)

def layer(state, weights, block_ids, cosine, sine):
    gain_attn, qkv_weight, out_weight, gain_ffn, gate_up_weight, down_weight = weights
    length = state.shape[0]
    width_q = HEADS * HEAD_DIM
    width_k = KV_HEADS * HEAD_DIM
    normed = low(norm_rows(state, gain_attn))
    mixed = low_back(low(product(normed, qkv_weight)))
    queries = mixed[:, :width_q].reshape(length, HEADS, HEAD_DIM)
    keys = mixed[:, width_q:width_q + width_k].reshape(length, KV_HEADS, HEAD_DIM)
    values = mixed[:, width_q + width_k:].reshape(length, KV_HEADS, HEAD_DIM)
    queries = low(rotate(queries, cosine, sine))
    keys = low(rotate(keys, cosine, sine))
    attended = low_back(low(attend(queries, keys, values, block_ids)))
    hidden = state + low_back(product(attended, out_weight))
    normed_ffn = low(norm_rows(hidden, gain_ffn))
    gated = low_back(low(product(normed_ffn, gate_up_weight.reshape(D, 2 * FF)))).reshape(length, 2, FF)
    inner = low(jax.nn.silu(gated[:, 0]) * gated[:, 1])
    return hidden + low_back(product(inner, down_weight))

def reference(layer_input, block_ids, positions, norm_attn, w_qkv, w_out, norm_ffn, w_gate_up, w_down, cotangent):
    params = (norm_attn.astype(jnp.float32), w_qkv.astype(jnp.float32), w_out.astype(jnp.float32), norm_ffn.astype(jnp.float32), w_gate_up.astype(jnp.float32), w_down.astype(jnp.float32))
    inputs = layer_input.astype(jnp.float32).reshape(N_DP, SEQ, D)
    cotangents = cotangent.astype(jnp.float32).reshape(N_DP, SEQ, D)

    def network(weights, start, seq_ids, cosine, sine):
        state = start
        for layer_index in range(LAYERS):
            state = layer(state, tuple((w_item[layer_index] for w_item in weights)), seq_ids, cosine, sine)
        return state

    def one_sequence(totals, seq_item):
        start, seq_cot, seq_ids, seq_pos = seq_item
        cosine, sine = angles(seq_pos)
        result, pull = jax.vjp(lambda weights, begin: network(weights, begin, seq_ids, cosine, sine), params, start)
        weight_grads, start_grad = pull(seq_cot)
        totals = tuple((total + grad_item for total, grad_item in zip(totals, weight_grads)))
        return (totals, (result.astype(jnp.bfloat16), start_grad))
    zeros = tuple((jnp.zeros(p_item.shape, jnp.float32) for p_item in params))
    totals, (results, start_grads) = lax.scan(one_sequence, zeros, (inputs, cotangents, block_ids, positions))
    return (results.reshape(N_DP * SEQ, D), start_grads.reshape(N_DP * SEQ, D), totals[0], totals[1], totals[2], totals[3], totals[4], totals[5])
```

```python
import jax
import jax.numpy as jnp
from jax import lax
from jax.sharding import PartitionSpec as P

D = 1152
HEADS = 18
KV_HEADS = 6
HEAD_DIM = 64
GROUP = HEADS // KV_HEADS
WQ = HEADS * HEAD_DIM
WK = KV_HEADS * HEAD_DIM
N_ROW = 4
N_COL = 4
PAIR = 2
CORES = 2
PLANE = PAIR * N_COL

epsilon = 1e-05
rope_base = 10000.0
bf16 = jnp.bfloat16
f32 = jnp.float32


def dot(left, right, dims=((1,), (0,))):
    return lax.dot_general(left, right, (dims, ((), ())), preferred_element_type=f32)


NT = ((1,), (1,))
TN = ((0,), (0,))


def plane_swap(value, mask):
    n_dp = lax.axis_size("dp")
    pairs = []
    for d in range(n_dp):
        for c in range(N_COL):
            pairs.append((d * N_COL + c, (d ^ (mask // N_COL)) * N_COL + (c ^ (mask % N_COL))))
    return lax.ppermute(value, ("dp", "col"), pairs)


def row_shift(value, step):
    return lax.ppermute(value, "row", [(r, (r + step) % N_ROW) for r in range(N_ROW)])


CHIPS = (0, 2, 4, 6)


def plane_gather(value):
    near = [value] + [plane_swap(value, m) for m in CHIPS[1:]]
    far = [plane_swap(piece, 1) for piece in near]
    return {m: near[i] for i, m in enumerate(CHIPS)} | {m + 1: far[i] for i, m in enumerate(CHIPS)}


def plane_reduce(pieces):
    far = [plane_swap(pieces[m + 1], 1) for m in CHIPS]
    summed = [pieces[m].astype(f32) + far[i].astype(f32) for i, m in enumerate(CHIPS)]
    total = summed[0]
    for i, m in enumerate(CHIPS[1:]):
        total = total + plane_swap(summed[i + 1].astype(bf16), m).astype(f32)
    return total


def tokens_in(value, own_row):
    n = value.shape[0] // N_ROW
    parts = value.reshape(N_ROW, n, value.shape[1])
    out = jnp.zeros((N_ROW, n, value.shape[1]), value.dtype)
    out = lax.dynamic_update_index_in_dim(out, lax.dynamic_index_in_dim(parts, own_row, 0, False), own_row, 0)
    for step in range(1, N_ROW):
        sent = lax.dynamic_index_in_dim(parts, (own_row + step) % N_ROW, 0, False)
        out = lax.dynamic_update_index_in_dim(out, row_shift(sent, step), (own_row - step) % N_ROW, 0)
    return jnp.transpose(out, (1, 0, 2)).reshape(n, N_ROW * value.shape[1])


def tokens_out(value, own_row):
    n, w = value.shape[0], value.shape[1] // N_ROW
    parts = jnp.transpose(value.reshape(n, N_ROW, w), (1, 0, 2))
    out = jnp.zeros((N_ROW, n, w), value.dtype)
    out = lax.dynamic_update_index_in_dim(out, lax.dynamic_index_in_dim(parts, own_row, 0, False), own_row, 0)
    for step in range(1, N_ROW):
        sent = lax.dynamic_index_in_dim(parts, (own_row + step) % N_ROW, 0, False)
        out = lax.dynamic_update_index_in_dim(out, row_shift(sent, step), (own_row - step) % N_ROW, 0)
    return out.reshape(N_ROW * n, w)


def sequence_gather(value):
    line = [value] + [row_shift(value, step) for step in range(1, N_ROW)]
    line = jnp.stack(line, 0)
    pair = jnp.concatenate([line, plane_swap(line, 2)], 0)
    return jnp.concatenate([pair, plane_swap(pair, 1)], 0)


def sequence_reduce(terms):
    half = terms.shape[0] // 2
    pair = terms[:half].astype(f32) + plane_swap(terms[half:], 1).astype(f32)
    line = pair[: half // 2] + plane_swap(pair[half // 2 :].astype(bf16), 2).astype(f32)
    total = line[0]
    for step in range(1, N_ROW):
        total = total + row_shift(line[step].astype(bf16), N_ROW - step).astype(f32)
    return total


def sequence_order(own_row, own_col):
    rows = (own_row - jnp.arange(N_ROW)) % N_ROW
    cols = jnp.stack([own_col, own_col ^ 2, own_col ^ 1, own_col ^ 3])
    return cols[:, None] * N_ROW + rows[None, :]


def norm_scale(state):
    return lax.rsqrt(jnp.mean(state * state, axis=1, keepdims=True) + epsilon)


def norm_backward(state, scale, gain, grad_normed, grad_state):
    inner = jnp.sum(state * gain * grad_normed, axis=1, keepdims=True)
    gain_grad = jnp.sum(state * scale * grad_normed, axis=0)
    state_grad = grad_state + scale * gain * grad_normed - state * (scale**3 * inner / D)
    return (state_grad, gain_grad)


def angles(positions):
    freq_index = jnp.arange(HEAD_DIM // 2).astype(f32)
    freqs = rope_base ** (-2.0 * freq_index / HEAD_DIM)
    phase = positions.astype(f32)[:, None] * freqs[None, :]
    phase = jnp.concatenate([phase, phase], axis=-1)
    return (jnp.cos(phase)[:, None, :], jnp.sin(phase)[:, None, :])


def rotate(values, cosine, sine):
    half_dim = values.shape[-1] // 2
    turned = jnp.concatenate([-values[..., half_dim:], values[..., :half_dim]], axis=-1)
    return values * cosine + turned * sine


def attend_forward(queries, keys, values, allowed):
    factor = HEAD_DIM ** (-0.5)
    key_heads = keys.reshape(-1, KV_HEADS, HEAD_DIM)
    value_heads = values.reshape(-1, KV_HEADS, HEAD_DIM)
    scores = jnp.einsum("hqd,khd->hqk", queries, key_heads, preferred_element_type=f32) * factor
    scores = jnp.where(allowed[None], scores, -1e30)
    row_max = jnp.max(scores, axis=-1, keepdims=True)
    weights = jnp.exp(scores - row_max)
    total = jnp.sum(weights, axis=-1, keepdims=True)
    out = jnp.einsum("hqk,khd->hqd", weights.astype(bf16), value_heads, preferred_element_type=f32)
    return out / total, row_max + jnp.log(total)


def attend_backward(queries, keys, values, allowed, attended, log_total, grad_attended):
    factor = HEAD_DIM ** (-0.5)
    key_heads = keys.reshape(-1, KV_HEADS, HEAD_DIM)
    value_heads = values.reshape(-1, KV_HEADS, HEAD_DIM)
    delta = jnp.sum(grad_attended.astype(f32) * attended, axis=-1, keepdims=True)
    scores = jnp.einsum("hqd,khd->hqk", queries, key_heads, preferred_element_type=f32) * factor
    weights = jnp.where(allowed[None], jnp.exp(scores - log_total), 0.0)
    dots = jnp.einsum("hqd,khd->hqk", grad_attended, value_heads, preferred_element_type=f32)
    slope = (weights * (dots - delta)).astype(bf16)
    grad_query = jnp.einsum("hqk,khd->hqd", slope, key_heads, preferred_element_type=f32) * factor
    grad_key = jnp.einsum("hqk,hqd->khd", slope, queries, preferred_element_type=f32) * factor
    grad_value = jnp.einsum("hqk,hqd->khd", weights.astype(bf16), grad_attended, preferred_element_type=f32)
    return grad_query, grad_key.reshape(-1, WK), grad_value.reshape(-1, WK)


def to_heads(values):
    n = values.shape[0]
    grouped = values.reshape(n, KV_HEADS, GROUP, HEAD_DIM)
    return jnp.transpose(grouped, (1, 2, 0, 3)).reshape(KV_HEADS, GROUP * n, HEAD_DIM)


def from_heads(values):
    n = values.shape[1] // GROUP
    grouped = values.reshape(KV_HEADS, GROUP, n, HEAD_DIM)
    return jnp.transpose(grouped, (2, 0, 1, 3)).reshape(n, WQ)


def split_heads(values, count):
    return values.reshape(values.shape[0], count, HEAD_DIM)


def layer_forward(state, weights, allowed, cosine, sine):
    gain_attn, qkv_weight, out_weight, gain_ffn, mlp_weight = weights
    n = state.shape[0]
    ff = mlp_weight.shape[1] // 3
    scale_attn = norm_scale(state)
    normed = (state * scale_attn * gain_attn).astype(bf16)
    mixed = dot(normed, qkv_weight, NT).astype(bf16)
    keys = rotate(split_heads(mixed[:, WQ : WQ + WK].astype(f32), KV_HEADS), cosine, sine)
    keys = keys.astype(bf16).reshape(n, WK)
    keys_all = sequence_gather(keys).reshape(-1, WK)
    values_all = sequence_gather(mixed[:, WQ + WK :]).reshape(-1, WK)
    queries = rotate(split_heads(mixed[:, :WQ].astype(f32), HEADS), cosine, sine)
    queries = to_heads(queries.astype(bf16).reshape(n, WQ))
    attended, log_total = attend_forward(queries, keys_all, values_all, allowed)
    attended_b = from_heads(attended.astype(bf16))
    hidden = state + dot(attended_b, out_weight)
    scale_ffn = norm_scale(hidden)
    normed_ffn = (hidden * scale_ffn * gain_ffn).astype(bf16)
    pieces = plane_gather(normed_ffn)
    normed_all = jnp.concatenate([pieces[m] for m in range(PLANE)], 0)
    gated = dot(normed_all, mlp_weight[:, : 2 * ff]).astype(bf16)
    inner = (jax.nn.silu(gated[:, :ff].astype(f32)) * gated[:, ff:].astype(f32)).astype(bf16)
    term = dot(inner, mlp_weight[:, 2 * ff :], NT).astype(bf16)
    down = plane_reduce([term[m * n : (m + 1) * n] for m in range(PLANE)])
    record = dict(
        state=state, scale_attn=scale_attn, normed=normed, queries=queries, keys_all=keys_all,
        values_all=values_all, attended=attended, attended_b=attended_b, log_total=log_total,
        hidden=hidden, scale_ffn=scale_ffn, normed_all=normed_all, gated=gated, inner=inner,
    )
    return (record, hidden + down)


def layer_backward(grad_state, record, weights, allowed, cosine, sine, slots):
    gain_attn, qkv_weight, out_weight, gain_ffn, mlp_weight = weights
    n = grad_state.shape[0]
    ff = mlp_weight.shape[1] // 3
    pieces = plane_gather(grad_state.astype(bf16))
    grad_all = jnp.concatenate([pieces[m] for m in range(PLANE)], 0)
    grad_inner = dot(grad_all, mlp_weight[:, 2 * ff :])
    gate = record["gated"][:, :ff].astype(f32)
    up = record["gated"][:, ff:].astype(f32)
    sig = jax.nn.sigmoid(gate)
    grad_gate = grad_inner * up * sig * (1.0 + gate * (1.0 - sig))
    grad_up = grad_inner * gate * sig
    grad_gated = jnp.concatenate([grad_gate, grad_up], axis=1).astype(bf16)
    term = dot(grad_gated, mlp_weight[:, : 2 * ff], NT).astype(bf16)
    grad_normed = plane_reduce([term[m * n : (m + 1) * n] for m in range(PLANE)])
    grad_mlp = jnp.concatenate(
        [dot(record["normed_all"], grad_gated, TN), dot(grad_all, record["inner"], TN)], axis=1
    ).astype(bf16)
    grad_mlp = lax.psum_scatter(grad_mlp, "row", scatter_dimension=0, tiled=True)
    grad_hidden, gain_ffn_grad = norm_backward(
        record["hidden"], record["scale_ffn"], gain_ffn, grad_normed, grad_state
    )
    grad_branch = grad_hidden.astype(bf16)
    grad_out = dot(record["attended_b"], grad_branch, TN).astype(bf16)
    grad_attended = to_heads(dot(grad_branch, out_weight, NT).astype(bf16))
    grad_query, key_terms, value_terms = attend_backward(
        record["queries"], record["keys_all"], record["values_all"], allowed,
        record["attended"], record["log_total"], grad_attended,
    )
    blocks = N_ROW * N_COL
    key_grad = sequence_reduce(key_terms.astype(bf16).reshape(blocks, n, WK))
    value_grad = sequence_reduce(value_terms.astype(bf16).reshape(blocks, n, WK))
    grad_query = rotate(split_heads(from_heads(grad_query), HEADS), cosine, -sine).reshape(n, WQ)
    key_grad = rotate(split_heads(key_grad, KV_HEADS), cosine, -sine).reshape(n, WK)
    grad_mixed = jnp.concatenate([grad_query, key_grad, value_grad], axis=1).astype(bf16)
    grad_normed = dot(grad_mixed, qkv_weight)
    grad_qkv = dot(grad_mixed, record["normed"], TN).astype(bf16)
    grad_input, gain_attn_grad = norm_backward(
        record["state"], record["scale_attn"], gain_attn, grad_normed, grad_hidden
    )

    def scatter_attn(full):
        parts = full.reshape(PLANE, -1, D)
        mine = plane_reduce([lax.dynamic_index_in_dim(parts, slots[m], 0, False) for m in range(PLANE)])
        return lax.psum_scatter(mine.astype(bf16).T, "row", scatter_dimension=0, tiled=True)

    return (grad_input, (gain_attn_grad, gain_ffn_grad, scatter_attn(grad_qkv), scatter_attn(grad_out), grad_mlp))


def both_halves(half_grad, own_half):
    n_dp = lax.axis_size("dp")
    total = half_grad
    for step in range(1, n_dp // PAIR):
        other = lax.ppermute(half_grad, "dp", [(d, (d + PAIR * step) % n_dp) for d in range(n_dp)])
        total = (total.astype(f32) + other.astype(f32)).astype(bf16)
    other = plane_swap(total, N_COL)
    return jnp.where(own_half == 0, jnp.stack([total, other]), jnp.stack([other, total]))


def local(layer_input, block_ids, positions, norm_attn, w_qkv, w_out, norm_ffn, w_gate_up, w_down, cotangent):
    layers = w_qkv.shape[0]
    own_row = lax.axis_index("row")
    own_col = lax.axis_index("col")
    own_half = lax.axis_index("dp") % PAIR
    slot = own_col * PAIR + own_half
    slots = [(own_col ^ (m % N_COL)) * PAIR + (own_half ^ (m // N_COL)) for m in range(PLANE)]

    def take_half(value, axis):
        size = value.shape[axis] // PAIR
        return lax.dynamic_slice_in_dim(value, own_half * size, size, axis)

    attn_parts = []
    mlp_parts = []
    for i in range(layers):
        attn_part = jnp.concatenate([take_half(w_qkv[i], 1).T, take_half(w_out[i], 0)], 0)
        attn_parts.append(attn_part)
        gate_up = take_half(w_gate_up[i], 2).reshape(w_gate_up.shape[1], -1)
        mlp_parts.append(jnp.concatenate([gate_up, take_half(w_down[i], 0).T], 1))
    tokens = jnp.concatenate([block_ids, positions], 0)
    tokens_all = lax.all_gather(tokens, ("row", "col"), axis=1, tiled=True)
    state_in = tokens_in(layer_input, own_row)
    gains = lax.all_gather(jnp.concatenate([norm_attn, norm_ffn], 0), "row", axis=1, tiled=True)

    rows_qkv = w_qkv.shape[2] // PAIR
    layer_weights = []
    for i in range(layers):
        piece = lax.all_gather(attn_parts[i], "row", axis=1, tiled=True)
        mlp_weight = lax.all_gather(mlp_parts[i], "row", axis=0, tiled=True)
        pieces = plane_gather(piece)
        qkv_weight = jnp.zeros((PLANE, rows_qkv, D), bf16)
        out_weight = jnp.zeros((PLANE, piece.shape[0] - rows_qkv, D), bf16)
        for m in range(PLANE):
            qkv_weight = lax.dynamic_update_index_in_dim(qkv_weight, pieces[m][:rows_qkv], slots[m], 0)
            out_weight = lax.dynamic_update_index_in_dim(out_weight, pieces[m][rows_qkv:], slots[m], 0)
        layer_weights.append(
            (gains[i], qkv_weight.reshape(-1, D), out_weight.reshape(-1, D), gains[layers + i], mlp_weight)
        )

    n = state_in.shape[0]
    blocks = tokens_all.reshape(2, N_ROW * N_COL, n)
    own = lax.dynamic_index_in_dim(blocks, own_col * N_ROW + own_row, 1, False)
    ids_own = own[0]
    cosine, sine = angles(own[1])
    ids_all = blocks[0][sequence_order(own_row, own_col).reshape(-1)].reshape(-1)
    allowed = ids_all[None, :] <= ids_own[:, None]
    allowed = jnp.tile(allowed, (GROUP, 1))

    state = state_in.astype(f32)
    records = []
    for i in range(layers):
        record, state = layer_forward(state, layer_weights[i], allowed, cosine, sine)
        records.append(record)
    result = tokens_out(state.astype(bf16), own_row)
    grad_state = tokens_in(cotangent, own_row).astype(f32)
    collected = [None] * layers
    for i in reversed(range(layers)):
        grad_state, collected[i] = layer_backward(
            grad_state, records[i], layer_weights[i], allowed, cosine, sine, slots
        )
    input_grad = tokens_out(grad_state.astype(bf16), own_row).astype(f32)

    gain_grads = jnp.stack([collected[i][0] for i in range(layers)] + [collected[i][1] for i in range(layers)])
    gain_grads = lax.psum(gain_grads, ("dp", "row", "col"))
    gain_grads = lax.dynamic_slice_in_dim(gain_grads, own_row * (D // N_ROW), D // N_ROW, 1)

    qkv_grads, out_grads, gate_up_grads, down_grads = [], [], [], []
    width = D // N_ROW
    for i in range(layers):
        qkv = both_halves(collected[i][2], own_half)
        qkv_grads.append(jnp.transpose(qkv, (1, 0, 2)).reshape(width, -1))
        out = both_halves(collected[i][3], own_half)
        out_grads.append(jnp.transpose(out, (0, 2, 1)).reshape(-1, width))
        mlp = both_halves(collected[i][4], own_half)
        ff = mlp.shape[2] // 3
        gate_up = mlp[:, :, : 2 * ff].reshape(PAIR, width, 2, ff)
        gate_up_grads.append(jnp.transpose(gate_up, (1, 2, 0, 3)).reshape(width, 2, PAIR * ff))
        down_grads.append(jnp.transpose(mlp[:, :, 2 * ff :], (0, 2, 1)).reshape(-1, width))
    return (
        result,
        input_grad,
        gain_grads[:layers],
        jnp.stack(qkv_grads).astype(f32),
        jnp.stack(out_grads).astype(f32),
        gain_grads[layers:],
        jnp.stack(gate_up_grads).astype(f32),
        jnp.stack(down_grads).astype(f32),
    )


def solution(mesh):
    in_specs = (
        P(("dp", "col"), "row"),
        P("dp", ("row", "col")),
        P("dp", ("row", "col")),
        P(None, "row"),
        P(None, "row", "col"),
        P(None, "col", "row"),
        P(None, "row"),
        P(None, "row", None, "col"),
        P(None, "col", "row"),
        P(("dp", "col"), "row"),
    )
    out_specs = (
        P(("dp", "col"), "row"),
        P(("dp", "col"), "row"),
        P(None, "row"),
        P(None, "row", "col"),
        P(None, "col", "row"),
        P(None, "row"),
        P(None, "row", None, "col"),
        P(None, "col", "row"),
    )
    return jax.shard_map(local, mesh=mesh, in_specs=in_specs, out_specs=out_specs, check_vma=False)
```
